32 devices in a mesh: dp: 16 (over z, y, x), tensor: 2 (over core).
Axes of the slice: x: 2, y: 2, z: 4, core: 2. Of those that a mesh axis runs over, the one named last changes fastest.
Arguments:
- token_ids: int32 [16384], replicated, may hold values from 0 to 50303
- segment_ids: int32 [16384], P('dp'), may hold values from 0 to 127, never falling along the last dimension, each value on 1 to 1024 neighbouring positions
- routes: int32 [16384, 4], P('dp'), may hold values from 0 to 15, all different within a row; in each aligned block of 1024 rows (0 to 1023, 1024 to 2047, ...) at most 384 rows name the same one
- loss_rows: int32 [2048], replicated, may hold values from 0 to 1022, as said below
- valid_mask: int32 [2048], replicated, may hold values from 0 to 1, as said below
- step_count: int32 [1], replicated, may hold values from 1 to 20
- emb_w: float32 [50304, 1024], P(None, 'dp'), may hold values from -6 to 6
- emb_m: float32 [50304, 1024], P(None, 'dp'), may hold values from -9.765625e-06 to 9.765625e-06
- emb_v: float32 [50304, 1024], P(None, 'dp'), may hold values from 2.3841857e-12 to 2.3841857e-11
- head_w: float32 [50304, 1024], P(('dp', 'tensor')), may hold values from -6 to 6
- head_m: float32 [50304, 1024], P(('dp', 'tensor')), may hold values from -9.765625e-06 to 9.765625e-06
- head_v: float32 [50304, 1024], P(('dp', 'tensor')), may hold values from 2.3841857e-12 to 2.3841857e-11
- att_w: float32 [1024, 4, 1024], P('dp', None, 'tensor'), may hold values from -6 to 6
- att_mom: float32 [1024, 4, 1024], P('dp', None, 'tensor'), may hold values from -0.00044194172 to 0.00044194172
- exp_w: float32 [16, 3, 1024, 512], P('dp', None, None, 'tensor'), may hold values from -6 to 6
- exp_mom: float32 [16, 3, 1024, 512], P('dp', None, None, 'tensor'), may hold values from -0.00015467961 to 0.00015467961
- small_w: float32 [1024, 21], P('dp'), may hold values from -4 to 4, as said below
- small_m: float32 [1024, 21], P('dp'), may hold values from -0.00030935922 to 0.00030935922
- small_v: float32 [1024, 21], P('dp'), may hold values from 2.4414062e-09 to 2.4414062e-08
Outputs:
- loss: float32 [], replicated
- grad_norm: float32 [], replicated
- emb_update: float32 [50304, 1024], P(None, 'dp')
- emb_m_out: float32 [50304, 1024], P(None, 'dp')
- emb_v_out: float32 [50304, 1024], P(None, 'dp')
- emb_low_out: bfloat16 [50304, 1024], P(None, 'dp')
- head_update: float32 [50304, 1024], P(('dp', 'tensor'))
- head_m_out: float32 [50304, 1024], P(('dp', 'tensor'))
- head_v_out: float32 [50304, 1024], P(('dp', 'tensor'))
- head_low_out: bfloat16 [50304, 1024], P(('dp', 'tensor'))
- att_update: float32 [1024, 4, 1024], P('dp', None, 'tensor')
- att_mom_out: float32 [1024, 4, 1024], P('dp', None, 'tensor')
- att_low_out: bfloat16 [1024, 4, 1024], P('dp', None, 'tensor')
- exp_update: float32 [16, 3, 1024, 512], P('dp', None, None, 'tensor')
- exp_mom_out: float32 [16, 3, 1024, 512], P('dp', None, None, 'tensor')
- exp_low_out: bfloat16 [16, 3, 1024, 512], P('dp', None, None, 'tensor')
- small_update: float32 [1024, 21], P('dp')
- small_m_out: float32 [1024, 21], P('dp')
- small_v_out: float32 [1024, 21], P('dp')
- small_low_out: bfloat16 [1024, 21], P('dp')
The draws below stay inside these ranges and needn't reach their ends.
Inputs may be any that keep to these rules, and one draw needn't show every extreme that they name: `routes`: in each aligned block of 1024 rows no expert is named by more than 384 rows, a bound that some block reaches. `loss_rows`: in each aligned block of 128 entries the positions are distinct, and each block holds 0 and 1022. `valid_mask`: the first entry is 1. `small_w`: gain columns are positive.
All inputs are finite; a program needn't handle non-finite values.
Results may differ from the reference program's by a relative error of at most 0.009.
Values may be sent and summed in bfloat16 or wider, within the bound.
No kernel may reach another device: no remote copies, remote signals or barrier semaphores. Data moves between devices by JAX's collectives and lax.ppermute only.
A program may use at most 448 MiB of HBM per device.

```python
import math
import jax
import jax.numpy as jnp
import numpy as np
from jax import lax

D = 1024
H = 16
HD = 64
FE = 512
V = 50304
TOP = 4
DOCS = 8
TOK_DEV = 1024
LOSS_DEV = 128
EXPERTS = 16
CAP = 384
TOKENS = 16384
NLOSS = 2048
GW = 512
FH = 256
N_DP = 16
N_TENSOR = 2


def draw_loss_rows(key, part):
    keys = jax.random.split(key, N_DP)

    def one_block(block_key):
        inner = jax.random.permutation(block_key, TOK_DEV - 3) + 1
        ends = jnp.array([0, TOK_DEV - 2], dtype=jnp.int32)
        return jnp.concatenate([ends, inner[:LOSS_DEV - 2].astype(jnp.int32)])
    return jax.vmap(one_block)(keys).reshape(NLOSS).astype(jnp.int32)


def draw_valid_mask(key, part):
    levels = jax.random.randint(key, (NLOSS,), 0, 4)
    marks = (levels > 0).astype(jnp.int32)
    return marks.at[0].set(1)


def draw_small_w(key, part):
    first_key, second_key = jax.random.split(key)
    router = jnp.clip(jax.random.normal(first_key, (D, EXPERTS), jnp.float32), -4.0, 4.0)
    gains = jnp.clip(1.0 + 0.15 * jax.random.normal(second_key, (D, 5), jnp.float32), 0.5, 1.5)
    return jnp.concatenate([router, gains], axis=1).astype(jnp.float32)


def place_ends(result, own_key, low, top_value):
    shape = result.shape
    index_at = [jax.random.randint(jax.random.fold_in(own_key, axis), (), 0, shape[axis]) for axis in range(len(shape))]
    result = result.at[tuple(index_at)].set(low)
    longest = shape.index(max(shape))
    index_at[longest] = (index_at[longest] + 1) % shape[longest]
    return result.at[tuple(index_at)].set(top_value)


def block_levels(own_key, shape, cuts, smallest, high):
    level = 1.0
    for axis_at, shards_of in cuts:
        draws = jax.random.uniform(jax.random.fold_in(jax.random.fold_in(own_key, 6), axis_at), (shards_of,), jnp.float32, smallest / len(cuts), high / len(cuts))
        level = level * jnp.repeat(jnp.exp(draws), shape[axis_at] // shards_of).reshape((-1,) + (1,) * (len(shape) - 1 - axis_at))
    return level


def rank_bounds(amount, lean):
    portions = [(1 << 20) // math.isqrt(standing ** lean) + 1 for standing in range(1, amount + 1)]
    deviation = 1 + sum(portions) // (1 << 30)
    return np.cumsum(np.array([max(1, weight // deviation) for weight in portions]))


def ranked_ids(key, shape, count, skew):
    grid = rank_bounds(count, skew)
    ticket = jax.random.randint(jax.random.fold_in(key, 1), shape, 0, int(grid[count - 1]))
    standing = jnp.searchsorted(jnp.asarray(grid, jnp.int32), ticket, side="right")
    return jax.random.permutation(jax.random.fold_in(key, 2), count)[standing].astype(jnp.int32)


def length_profile(number_of, total, bound, slope):
    portions = [(1 << 20) // math.isqrt(grade ** slope) + 1 for grade in range(2, number_of + 1)]
    surplus, holding = total - bound - (number_of - 1), [1] * (number_of - 1)
    while surplus > 0:
        movable = [i for i in range(number_of - 1) if holding[i] < bound]
        pool, budget = sum([portions[i] for i in movable]), surplus
        for i in movable:
            extra = min(bound - holding[i], max(1, budget * portions[i] // pool), surplus)
            holding[i] = holding[i] + extra
            surplus = surplus - extra
    return np.array([bound] + holding)


def ragged_sizes(key, amount, total, reach, slope):
    if amount == 2:
        one = jax.random.randint(key, (), max(1, total - reach), min(reach, total - 1) + 1)
        return jnp.stack([one, total - one])
    tallies = jnp.asarray(length_profile(amount, total, reach, slope), jnp.int32)
    pairs = (amount - 1) // 2
    donor, receiver = tallies[1:1 + 2 * pairs:2], tallies[2:2 + 2 * pairs:2]
    room = jnp.minimum(donor - 1, reach - receiver)
    moved = jax.random.randint(jax.random.fold_in(key, 1), (pairs,), 0, 1 << 20) % (room + 1)
    tallies = tallies.at[1:1 + 2 * pairs:2].set(donor - moved).at[2:2 + 2 * pairs:2].set(receiver + moved)
    return tallies[jax.random.permutation(jax.random.fold_in(key, 2), amount)]


def assign_block(own_key, own, number, rows, count, top, limit, skew):
    order = jax.random.permutation(own_key, count)
    packed, ordinary = shares(count, rows * top, limit, skew, True), shares(count, rows * top, limit, skew, False)
    places = jnp.arange(count)

    def named(sizes, rotation):
        used = int((sizes > 0).sum())
        fixed = max(1, used // 4)
        passed = fixed + (places - fixed + rotation * (used - fixed)) % max(1, count - fixed)
        return jnp.zeros((count,), jnp.int32).at[order[jnp.where(places < fixed, places, passed)]].set(jnp.asarray(sizes, jnp.int32))

    sizes = jnp.where(number % 4 == 0, named(packed, number // 4), named(ordinary, number - number // 4 - 1))
    mixed = jax.random.permutation(jax.random.fold_in(own, 3), count)
    giver, taker = mixed[0:count // 2 * 2:2], mixed[1:count // 2 * 2:2]
    room = jnp.minimum(sizes[giver] - 1, limit - sizes[taker]) // 2
    room = jnp.where((giver == order[0]) | (taker == order[0]) | (sizes[taker] == 0), 0, jnp.maximum(room, 0))
    passed = jax.random.randint(jax.random.fold_in(own, 4), (count // 2,), 0, 1 << 20) % (room + 1)
    sizes = sizes.at[giver].add(-passed).at[taker].add(passed)
    members = jnp.searchsorted(jnp.cumsum(sizes), jnp.arange(rows * top), side="right").astype(jnp.int32)
    listing = members.reshape(top, rows).T
    listing = listing[jax.random.permutation(jax.random.fold_in(own, 1), rows)]
    rotation = jax.random.randint(jax.random.fold_in(own, 2), (rows, 1), 0, top)
    return jnp.take_along_axis(listing, (jnp.arange(top)[None, :] + rotation) % top, axis=1)


def shares(count, total, limit, skew, full):
    loads = [(1 << 20) // math.isqrt(standing ** skew) + 1 for standing in range(1, count + 1)]
    largest = limit if full else min(limit, max(-(-total // count), total * loads[0] // sum(loads)))
    least = 1 if total - largest >= count - 1 else 0
    given, spare = [largest] + [least] * (count - 1), total - largest - least * (count - 1)
    while spare > 0:
        candidates = [i for i in range(1, count) if given[i] < largest] or [i for i in range(1, count) if given[i] < limit]
        whole, budget = sum([loads[i] for i in candidates]), spare
        for i in candidates:
            addition = min(limit - given[i], max(1, budget * loads[i] // whole), spare)
            given[i] = given[i] + addition
            spare = spare - addition
    return np.array(given)


def scatter_about(stream_key, dims, width, limit, shards=(), kind=jnp.bfloat16):
    drawn = jax.random.normal(stream_key, dims, jnp.float32) * width
    if len(shards) > 0:
        drawn = block_levels(stream_key, dims, shards, -0.22, 0.18) * drawn
    return jnp.clip(drawn, min=-limit, max=limit).astype(kind)


def setup_inputs(seed: int = 0) -> dict:
    key_list = jax.random.split(jax.random.key(seed), 20)
    token_ids = place_ends(ranked_ids(key_list[0], (TOKENS,), V, 2), jax.random.fold_in(key_list[0], 3), 0, V - 1).astype(jnp.int32)
    segment_ids = jnp.searchsorted(jnp.cumsum(ragged_sizes(key_list[1], DOCS * N_DP, TOKENS, TOK_DEV, 1)), jnp.arange(TOKENS), side="right").astype(jnp.int32)
    routes_keys = jax.random.split(jax.random.fold_in(key_list[2], 1), TOKENS // TOK_DEV)
    routes_turns = jax.random.permutation(jax.random.fold_in(key_list[2], 3), TOKENS // TOK_DEV)
    routes = jax.vmap(lambda own, number: assign_block(jax.random.fold_in(key_list[2], 2), own, number, TOK_DEV, EXPERTS, TOP, CAP, 1))(routes_keys, routes_turns).reshape((TOKENS, TOP))
    loss_rows = draw_loss_rows(jax.random.fold_in(key_list[19], 71), 0)
    valid_mask = draw_valid_mask(jax.random.fold_in(key_list[19], 71), 0)
    step_count = jax.random.randint(key_list[5], (1,), 1, 21).astype(jnp.int32)
    emb_w = scatter_about(key_list[6], (V, D), 1.0, 6.0, ((1, 16),), jnp.float32)
    emb_m = scatter_about(key_list[7], (V, D), (0.003 * NLOSS ** -1), 9.765624781721272e-06, ((1, 16),), jnp.float32)
    emb_v = jnp.clip(jnp.exp(math.log(2.384185730786026e-11) - 2.3025851 * jax.random.uniform(key_list[8], (V, D), jnp.float32) ** block_levels(key_list[8], (V, D), ((1, 16),), -0.2, 0.2)), 2.384185730786026e-12, 2.384185730786026e-11)
    head_w = scatter_about(key_list[9], (V, D), 1.0, 6.0, ((0, 32),), jnp.float32)
    head_m = scatter_about(key_list[10], (V, D), (0.003 * NLOSS ** -1), 9.765624781721272e-06, ((0, 32),), jnp.float32)
    head_v = jnp.clip(jnp.exp(math.log(2.384185730786026e-11) - 2.3025851 * jax.random.uniform(key_list[11], (V, D), jnp.float32) ** block_levels(key_list[11], (V, D), ((0, 32),), -0.2, 0.2)), 2.384185730786026e-12, 2.384185730786026e-11)
    att_w = scatter_about(key_list[12], (D, 4, D), 1.0, 6.0, ((0, 16), (2, 2)), jnp.float32)
    att_mom = scatter_about(key_list[13], (D, 4, D), (0.003 * NLOSS ** -0.5), 0.00044194172, ((0, 16), (2, 2)), jnp.float32)
    exp_w = scatter_about(key_list[14], (EXPERTS, 3, D, FE), 1.0, 6.0, ((0, 16), (3, 2)), jnp.float32)
    exp_mom = scatter_about(key_list[15], (EXPERTS, 3, D, FE), (0.001 * NLOSS ** -0.5), 0.00015467961, ((0, 16), (3, 2)), jnp.float32)
    small_w = draw_small_w(jax.random.fold_in(key_list[19], 71), 0)
    small_m = scatter_about(key_list[17], (D, EXPERTS + 5), (0.002 * NLOSS ** -0.5), 0.00030935922, ((0, 16),), jnp.float32)
    small_v = jnp.clip(jnp.exp(math.log(2.4414061883248905e-08) - 2.3025851 * jax.random.uniform(key_list[18], (D, EXPERTS + 5), jnp.float32) ** block_levels(key_list[18], (D, EXPERTS + 5), ((0, 16),), -0.2, 0.2)), 2.4414061883248905e-09, 2.4414061883248905e-08)
    return dict(token_ids=token_ids, segment_ids=segment_ids, routes=routes, loss_rows=loss_rows, valid_mask=valid_mask, step_count=step_count, emb_w=emb_w, emb_m=emb_m, emb_v=emb_v, head_w=head_w, head_m=head_m, head_v=head_v, att_w=att_w, att_mom=att_mom, exp_w=exp_w, exp_mom=exp_mom, small_w=small_w, small_m=small_m, small_v=small_v)


@jax.custom_vjp
def low(v):
    return lax.optimization_barrier(v.astype(jnp.bfloat16)).astype(jnp.float32)

@jax.custom_vjp
def low_back(v):
    return v

def low_keep(v):
    return (low(v), None)

def low_pass(kept, grad):
    return (grad,)

def back_keep(v):
    return (v, None)

def back_low(kept, grad):
    return (low(grad),)
low.defvjp(low_keep, low_pass)
low_back.defvjp(back_keep, back_low)
norm_epsilon = 1e-05
highest = lax.Precision.HIGHEST
poly_first = 3.4445
poly_second = -4.775
poly_third = 2.0315

def matmul(left, right):
    return jnp.dot(left, right, precision=highest, preferred_element_type=jnp.float32)

def rms_norm(values, gain):
    return values * lax.rsqrt(lax.optimization_barrier(jnp.mean(values * values, axis=-1, keepdims=True)) + norm_epsilon) * gain

def doc_positions(segments):
    places = jnp.arange(segments.shape[0], dtype=jnp.int32)
    change = jnp.concatenate([jnp.ones((1,), dtype=bool), segments[1:] != segments[:-1]])
    starts = lax.cummax(jnp.where(change, places, jnp.int32(0)), axis=0)
    return (places - starts).astype(jnp.float32)

def rotate(values, positions):
    half = values.shape[-1] // 2
    freq = 10000.0 ** (-2.0 * jnp.arange(half, dtype=jnp.float32) / values.shape[-1])
    angle = positions[:, None] * freq[None, :]
    cosine = jnp.cos(angle)[:, None, :]
    sine = jnp.sin(angle)[:, None, :]
    first = values[..., :half]
    second = values[..., half:]
    return jnp.concatenate([first * cosine - second * sine, second * cosine + first * sine], axis=-1)

def attend(rows, segments, att_low, gain_att, gain_q, gain_k):
    scale = D ** (-0.5)
    normed = low(rms_norm(rows, gain_att))
    query = low_back(matmul(normed, att_low[:, 0, :]) * scale).reshape(TOK_DEV, H, HD)
    keys = low_back(matmul(normed, att_low[:, 1, :]) * scale).reshape(TOK_DEV, H, HD)
    values = low_back(matmul(normed, att_low[:, 2, :]) * scale)
    positions = doc_positions(segments)
    query_rot = low(rotate(rms_norm(query, gain_q.reshape(H, HD)), positions))
    key_rot = low(rotate(rms_norm(keys, gain_k.reshape(H, HD)), positions))
    value_low = low(values).reshape(TOK_DEV, H, HD)
    places = jnp.arange(TOK_DEV, dtype=jnp.int32)
    block_rows = min(512, TOK_DEV)

    def block(start):
        q_block = lax.dynamic_slice_in_dim(query_rot, start, block_rows, 0)
        q_places = lax.dynamic_slice_in_dim(places, start, block_rows, 0)
        q_segments = lax.dynamic_slice_in_dim(segments, start, block_rows, 0)
        allowed = (places[None, :] <= q_places[:, None]) & (segments[None, :] == q_segments[:, None])
        scores = low_back(jnp.einsum('qhd,khd->hqk', q_block, key_rot, precision=highest) * HD ** (-0.5))
        scores = jnp.where(allowed[None], scores, -1e+30)
        probs = jax.nn.softmax(scores, axis=-1)
        return jnp.einsum('hqk,khd->qhd', low(probs), value_low, precision=highest)
    starts = (jnp.arange(TOK_DEV // block_rows) * block_rows).astype(jnp.int32)
    outs = lax.map(jax.checkpoint(block), starts)
    joined = low(low_back(outs.reshape(TOK_DEV, D)))
    return low_back(matmul(joined, att_low[:, 3, :].T) * (8.0 * scale))

def forward(emb, head, att, expert, small, token_ids, segment_ids, routes, loss_rows, valid_mask):
    scale = D ** (-0.5)
    emb_low = low(emb)
    head_low = low(head)
    att_low = low(att)
    exp_low = low(expert)
    small_low = low(small)
    router = small_low[:, :EXPERTS]
    gain_att = small_low[:, EXPERTS]
    gain_q = small_low[:, EXPERTS + 1]
    gain_k = small_low[:, EXPERTS + 2]
    gain_moe = small_low[:, EXPERTS + 3]
    gain_fin = small_low[:, EXPERTS + 4]
    embedded = low_back(emb_low[token_ids])

    def sequence(carry, pieces):
        return (carry, jax.checkpoint(attend)(pieces[0], pieces[1], att_low, gain_att, gain_q, gain_k))
    unused, branch = lax.scan(sequence, jnp.float32(0.0), (embedded.reshape(N_DP, TOK_DEV, D), segment_ids.reshape(N_DP, TOK_DEV)))
    hidden = embedded + branch.reshape(TOKENS, D)
    moe_in = low(rms_norm(hidden, gain_moe))
    router_logits = low_back(matmul(moe_in, router) * scale)
    probs = jax.nn.softmax(router_logits, axis=-1)
    flat_routes = routes.reshape(N_DP, TOK_DEV * TOP)
    hot = (flat_routes[:, :, None] == jnp.arange(EXPERTS, dtype=jnp.int32)[None, None, :]).astype(jnp.int32)
    slots = lax.optimization_barrier(jnp.sum(hot * (jnp.cumsum(hot, axis=1) - 1), axis=2))
    column = flat_routes * CAP + slots
    owner = (jnp.arange(TOKENS * TOP, dtype=jnp.int32) // TOP).reshape(N_DP, TOK_DEV * TOP)
    table = jnp.full((N_DP, EXPERTS * CAP), TOKENS, dtype=jnp.int32)
    table = table.at[jnp.arange(N_DP, dtype=jnp.int32)[:, None], column].set(owner)
    table = table.reshape(N_DP, EXPERTS, CAP).transpose(1, 0, 2).reshape(EXPERTS, N_DP * CAP)
    moe_pad = jnp.concatenate([moe_in, jnp.zeros((1, D), jnp.float32)], axis=0)
    probs_pad = jnp.concatenate([probs, jnp.zeros((1, EXPERTS), jnp.float32)], axis=0)

    def expert_step(total, pieces):
        weights, slot_tokens, expert_index = pieces
        rows = moe_pad[slot_tokens]
        gate_here = probs_pad[slot_tokens, expert_index]
        output = jnp.zeros((N_DP * CAP, D), jnp.float32)
        for group in range(N_TENSOR):
            lower = group * FH
            rows_group = low_back(rows)
            gate_val = low_back(matmul(rows_group, weights[0][:, lower:lower + FH]) * scale)
            up_val = low_back(matmul(rows_group, weights[1][:, lower:lower + FH]) * scale)
            middle = low(jax.nn.silu(gate_val) * up_val)
            output = output + low(low_back(matmul(middle, weights[2][:, lower:lower + FH].T) * FE ** (-0.5)))
        contrib = EXPERTS / TOP * gate_here[:, None] * output
        return (total.at[slot_tokens].add(contrib), None)
    total, unused_out = lax.scan(jax.checkpoint(expert_step), jnp.zeros((TOKENS + 1, D), jnp.float32), (exp_low, table, jnp.arange(EXPERTS, dtype=jnp.int32)))
    after = hidden + total[:TOKENS]
    final = low(rms_norm(after, gain_fin))
    global_rows = (jnp.arange(NLOSS, dtype=jnp.int32) // LOSS_DEV * TOK_DEV + loss_rows).astype(jnp.int32)
    chosen = final[global_rows]
    targets = token_ids[global_rows + 1]
    valid = valid_mask.astype(jnp.float32)
    count = jnp.sum(valid)
    loss_block_rows = min(512, NLOSS)

    def loss_block(start):
        rows = lax.dynamic_slice_in_dim(chosen, start, loss_block_rows, 0)
        wanted = lax.dynamic_slice_in_dim(targets, start, loss_block_rows, 0)
        logits = low_back(matmul(rows, head_low.T) * scale)
        peak = lax.optimization_barrier(jnp.max(logits, axis=-1, keepdims=True))
        lse = peak[:, 0] + jnp.log(lax.optimization_barrier(jnp.sum(jnp.exp(logits - peak), axis=-1)))
        picked = jnp.take_along_axis(logits, wanted[:, None], axis=1)[:, 0]
        return lse - picked
    loss_starts = (jnp.arange(NLOSS // loss_block_rows) * loss_block_rows).astype(jnp.int32)
    per_row = lax.map(jax.checkpoint(loss_block), loss_starts).reshape(NLOSS)
    return jnp.sum(valid * per_row) / count

def adam_step(weight, first, second, grad, count_t):
    first_new = 0.9 * first + 0.1 * grad
    second_new = 0.95 * second + 0.05 * grad * grad
    first_hat = first_new / (1.0 - jnp.power(0.9, count_t))
    second_hat = second_new / (1.0 - jnp.power(0.95, count_t))
    update = -0.3 * (first_hat / (jnp.sqrt(second_hat) + 1e-08) + 0.1 * weight)
    return (update, first_new, second_new, (weight + update).astype(jnp.bfloat16))

def orthogonalize(block):
    frob_norm = jnp.sqrt(lax.optimization_barrier(jnp.sum(block * block, axis=(-2, -1), keepdims=True))) + 1e-07
    current = block / frob_norm
    for iteration in range(5):
        square = jnp.einsum('...rc,...re->...ce', current, current, precision=highest)
        polynomial = poly_second * square + poly_third * jnp.einsum('...ce,...ef->...cf', square, square, precision=highest)
        current = poly_first * current + jnp.einsum('...rc,...ce->...re', current, polynomial, precision=highest)
    return current

def reference(token_ids, segment_ids, routes, loss_rows, valid_mask, step_count, emb_w, emb_m, emb_v, head_w, head_m, head_v, att_w, att_mom, exp_w, exp_mom, small_w, small_m, small_v):

    def objective(emb, head, att, expert, small):
        return forward(emb, head, att, expert, small, token_ids, segment_ids, routes, loss_rows, valid_mask)
    loss, pullback = jax.vjp(objective, emb_w, head_w, att_w, exp_w, small_w)
    emb_grad, head_grad, att_grad, exp_grad, small_grad = pullback(jnp.ones_like(loss))
    total_sq = jnp.sum(emb_grad * emb_grad) + jnp.sum(head_grad * head_grad) + jnp.sum(att_grad * att_grad) + jnp.sum(exp_grad * exp_grad) + jnp.sum(small_grad * small_grad)
    grad_norm = jnp.sqrt(total_sq)
    clip = jnp.minimum(1.0, 2.0 * NLOSS ** (-0.5) / (grad_norm + 1e-06))
    count_t = step_count[0].astype(jnp.float32)
    emb_out = adam_step(emb_w, emb_m, emb_v, clip * emb_grad, count_t)
    head_out = adam_step(head_w, head_m, head_v, clip * head_grad, count_t)
    small_out = adam_step(small_w, small_m, small_v, clip * small_grad, count_t)
    att_moment = 0.5 * att_mom + clip * att_grad
    att_blocks = att_moment.reshape(D, 4, N_TENSOR, GW).transpose(1, 2, 0, 3)
    att_ortho = orthogonalize(att_blocks).transpose(2, 0, 1, 3).reshape(D, 4, D)
    att_update = -0.3 * (D ** 0.5 * att_ortho + 0.1 * att_w)
    exp_moment = 0.5 * exp_mom + clip * exp_grad
    exp_blocks = exp_moment.reshape(EXPERTS, 3, D, N_TENSOR, FH).transpose(0, 1, 3, 2, 4)
    exp_ortho = orthogonalize(exp_blocks).transpose(0, 1, 3, 2, 4).reshape(EXPERTS, 3, D, FE)
    exp_update = -0.3 * (D ** 0.5 * exp_ortho + 0.1 * exp_w)
    return (loss, grad_norm, emb_out[0], emb_out[1], emb_out[2], emb_out[3], head_out[0], head_out[1], head_out[2], head_out[3], att_update, att_moment, (att_w + att_update).astype(jnp.bfloat16), exp_update, exp_moment, (exp_w + exp_update).astype(jnp.bfloat16), small_out[0], small_out[1], small_out[2], small_out[3])
```

```python
import jax
import jax.numpy as jnp
from jax import lax
from jax.sharding import PartitionSpec as P

HD = 64
FE = 512


norm_epsilon = 1e-05
highest = lax.Precision.HIGHEST
poly_first = 3.4445
poly_second = -4.775
poly_third = 2.0315
low = jnp.bfloat16
wide = jnp.float32


def swap_tensor(value):
    return lax.ppermute(value, "tensor", [(0, 1), (1, 0)])


def swap_dp(value, bit, size):
    return lax.ppermute(value, "dp", [(rank, rank ^ bit) for rank in range(size)])


def bits_of(size):
    bits = []
    bit = size // 2
    while bit:
        bits.append(bit)
        bit //= 2
    return bits


def gather_half(block, size):
    bits = bits_of(size)
    outer = bits[:-2]
    current = block[None]
    for bit in outer:
        current = jnp.concatenate([current[None], swap_dp(current, bit, size)[None]], axis=0)
        current = current.reshape((-1,) + block.shape)
    order = []
    for index in range(current.shape[0]):
        code = 0
        for step, bit in enumerate(outer):
            if (index >> step) & 1:
                code |= bit
        order.append(code)
    mid = block.shape[1] // 2
    first = current[:, :, :mid]
    second = current[:, :, mid:]
    hi, lo = bits[-2], bits[-1]
    first_hi = swap_dp(first, hi, size)
    second_lo = swap_dp(second, lo, size)
    first = jnp.stack([first, first_hi], axis=1)
    second = jnp.stack([second, second_lo], axis=1)
    first_lo = swap_dp(first, lo, size)
    second_hi = swap_dp(second, hi, size)
    first = jnp.stack([first, first_lo], axis=2)
    second = jnp.stack([second, second_hi], axis=1)
    whole = jnp.concatenate([first, second], axis=-1)
    positions = [order.index(code) for code in sorted(order)]
    if positions != list(range(len(order))):
        whole = jnp.concatenate([whole[p : p + 1] for p in positions], axis=0)
    return whole.reshape((size,) + block.shape)


def gather_rows(block, size, tensor_rank):
    half = block.shape[1] // 2
    mine = lax.dynamic_slice_in_dim(block, tensor_rank * half, half, 1)
    gathered = gather_half(mine, size)
    other = swap_tensor(gathered)
    gathered = gathered.reshape(-1, half)
    other = other.reshape(-1, half)
    first = jnp.where(tensor_rank == 0, gathered, other)
    second = jnp.where(tensor_rank == 0, other, gathered)
    return jnp.concatenate([first, second], axis=1)


def scatter_half(blocks, size):
    bits = bits_of(size)
    outer = bits[:-2]
    _, rows, cols = blocks.shape
    mid = cols // 2
    hi, lo = bits[-2], bits[-1]
    cube = blocks.reshape(size // 4, 2, 2, rows, cols)
    first = cube[..., :mid]
    second = cube[..., mid:]
    first_got = swap_dp(first[:, :, 1].astype(low), lo, size)
    second_got = swap_dp(second[:, 1].astype(low), hi, size)
    first = first[:, :, 0] + first_got.astype(wide)
    second = second[:, 0] + second_got.astype(wide)
    first_got = swap_dp(first[:, 1].astype(low), hi, size)
    second_got = swap_dp(second[:, 1].astype(low), lo, size)
    first = first[:, 0] + first_got.astype(wide)
    second = second[:, 0] + second_got.astype(wide)
    current = jnp.concatenate([first, second], axis=-1)
    for bit in reversed(outer):
        current = current.reshape(-1, 2, rows, cols)
        got = swap_dp(current[:, 1].astype(low), bit, size)
        current = current[:, 0] + got.astype(wide)
    return current.reshape(rows, cols)


def scatter_rows(partial, size, tensor_rank):
    half = partial.shape[1] // 2
    first, second = partial[:, :half], partial[:, half:]
    keep = jnp.where(tensor_rank == 0, first, second)
    send = jnp.where(tensor_rank == 0, second, first).astype(low)
    summed = keep + swap_tensor(send).astype(wide)
    mine = scatter_half(summed.reshape(size, -1, half), size)
    other = swap_tensor(mine)
    first = jnp.where(tensor_rank == 0, mine, other)
    second = jnp.where(tensor_rank == 0, other, mine)
    return jnp.concatenate([first, second], axis=1)


def pair_sum(value):
    short = value.astype(low)
    return short.astype(wide) + swap_tensor(short).astype(wide)


def pair_sum_wide(value):
    return value + swap_tensor(value)


def pair_join(value, tensor_rank, axis):
    other = swap_tensor(value)
    first = jnp.where(tensor_rank == 0, value, other)
    second = jnp.where(tensor_rank == 0, other, value)
    return jnp.concatenate([first, second], axis=axis)


def norm_parts(values):
    inverse = lax.rsqrt(jnp.mean(values * values, axis=-1, keepdims=True) + norm_epsilon)
    return (values * inverse, inverse)


def norm_back(scaled_in, inverse, gain, grad_out):
    weighted = grad_out * gain
    gain_grad = jnp.sum(scaled_in * grad_out, axis=0)
    grad_in = inverse * (
        weighted - scaled_in * jnp.mean(weighted * scaled_in, axis=-1, keepdims=True)
    )
    return (grad_in, gain_grad)


def doc_positions(segments):
    places = jnp.arange(segments.shape[0], dtype=jnp.int32)
    change = jnp.concatenate([jnp.ones((1,), dtype=bool), segments[1:] != segments[:-1]])
    starts = lax.cummax(jnp.where(change, places, jnp.int32(0)), axis=0)
    return ((places - starts).astype(jnp.float32), places)


def rotation_tables(positions, head_dim):
    half = head_dim // 2
    freq = 10000.0 ** (-2.0 * jnp.arange(half, dtype=jnp.float32) / head_dim)
    angle = positions[:, None] * freq[None, :]
    return (jnp.cos(angle)[:, None, :], jnp.sin(angle)[:, None, :])


def rotate(values, cosine, sine):
    half = values.shape[-1] // 2
    first = values[..., :half]
    second = values[..., half:]
    return jnp.concatenate(
        [first * cosine - second * sine, second * cosine + first * sine], axis=-1
    )


def gram_local(block):
    return jnp.einsum("rsc,rse->sce", block, block, precision=highest)


def orthogonal_rows(moment, gram_fn):
    raw_gram = gram_fn(moment)
    frob_norm = jnp.sqrt(jnp.trace(raw_gram, axis1=1, axis2=2)) + 1e-07
    orthogonal = moment / frob_norm[None, :, None]
    square = raw_gram / (frob_norm * frob_norm)[:, None, None]
    for iteration in range(5):
        polynomial = poly_second * square + poly_third * jnp.einsum(
            "sce,sef->scf", square, square, precision=highest
        )
        orthogonal = poly_first * orthogonal + jnp.einsum(
            "rsc,sce->rse", orthogonal, polynomial, precision=highest
        )
        if iteration < 4:
            square = gram_fn(orthogonal)
    return orthogonal


def adam_step(weight, first, second, grad, count_t):
    first_new = 0.9 * first + 0.1 * grad
    second_new = 0.95 * second + 0.05 * grad * grad
    first_hat = first_new / (1.0 - jnp.power(0.9, count_t))
    second_hat = second_new / (1.0 - jnp.power(0.95, count_t))
    update = -0.3 * (first_hat / (jnp.sqrt(second_hat) + 1e-08) + 0.1 * weight)
    return (update, first_new, second_new, (weight + update).astype(jnp.bfloat16))


def contract_first(left, right):
    return lax.dot_general(
        left, right, (((0,), (0,)), ((), ())), preferred_element_type=jnp.float32
    )


def contract_last(left, right):
    return lax.dot_general(
        left, right, (((1,), (1,)), ((), ())), preferred_element_type=jnp.float32
    )


def dot(left, right):
    return jnp.dot(left, right, preferred_element_type=jnp.float32)


def per_device(
    token_ids,
    segment_ids,
    routes,
    loss_rows,
    valid_mask,
    step_count,
    emb_w,
    emb_m,
    emb_v,
    head_w,
    head_m,
    head_v,
    att_w,
    att_mom,
    exp_w,
    exp_mom,
    small_w,
    small_m,
    small_v,
):
    dp_size = lax.axis_size("dp")
    tensor_size = lax.axis_size("tensor")
    dp_rank = lax.axis_index("dp")
    tensor_rank = lax.axis_index("tensor")
    tok_dev = segment_ids.shape[0]
    width = head_w.shape[1]
    top_count = routes.shape[1]
    expert_count = small_w.shape[1] - 5
    nloss = loss_rows.shape[0]
    loss_dev = nloss // dp_size
    group_width = att_w.shape[2]
    own_width = emb_w.shape[1]
    heads_local = group_width // HD
    vocab_local = head_w.shape[0]
    d_scale = width ** (-0.5)
    att_mult = 8.0 * d_scale
    att_scale = HD ** (-0.5)
    down_scale = FE ** (-0.5)
    moe_scale = expert_count / top_count
    tok_half = tok_dev // tensor_size
    row_own = att_w.shape[0]

    att_flat = att_w.astype(low).reshape(row_own, 4 * group_width)
    att_low = lax.all_gather(att_flat, "dp", axis=0, tiled=True)
    w_query = att_low[:, :group_width]
    w_key = att_low[:, group_width : 2 * group_width]
    w_value = att_low[:, 2 * group_width : 3 * group_width]
    w_out = att_low[:, 3 * group_width :]
    small_low = lax.all_gather(small_w.astype(low), "dp", axis=0, tiled=True)
    router_low = small_low[:, :expert_count]
    gains = small_low[:, expert_count:].astype(wide)
    gain_att = gains[:, 0]
    gain_q = lax.dynamic_slice_in_dim(
        gains[:, 1], tensor_rank * group_width, group_width, 0
    ).reshape(heads_local, HD)
    gain_k = lax.dynamic_slice_in_dim(
        gains[:, 2], tensor_rank * group_width, group_width, 0
    ).reshape(heads_local, HD)
    gain_moe = gains[:, 3]
    gain_fin = gains[:, 4]

    emb_low = emb_w.astype(low)
    half_ids = lax.dynamic_slice_in_dim(
        token_ids.reshape(dp_size, tok_dev), tensor_rank * tok_half, tok_half, 1
    ).reshape(-1)
    columns = jnp.take(emb_low, half_ids, axis=0)
    arrived = lax.all_to_all(columns, "dp", split_axis=0, concat_axis=1, tiled=True)
    embedded_low = pair_join(arrived, tensor_rank, 0)
    embedded = embedded_low.astype(wide)

    positions, places = doc_positions(segment_ids)
    my_rows = lax.dynamic_slice_in_dim(loss_rows, dp_rank * loss_dev, loss_dev, 0)
    row_hot = my_rows[:, None] == places[None, :]
    row_sel = row_hot.astype(low)
    row_positions = jnp.sum(jnp.where(row_hot, positions[None, :], 0.0), axis=1)
    row_segments = jnp.sum(jnp.where(row_hot, segment_ids[None, :], 0), axis=1)
    cosine, sine = rotation_tables(positions, HD)
    row_cosine, row_sine = rotation_tables(row_positions, HD)

    att_hat, att_inv = norm_parts(embedded)
    att_in = (att_hat * gain_att).astype(low)
    row_in = dot(row_sel, att_in).astype(low)
    row_embedded = dot(row_sel, embedded_low)
    query_raw = (dot(row_in, w_query) * d_scale).reshape(loss_dev, heads_local, HD)
    key_raw = (dot(att_in, w_key) * d_scale).reshape(tok_dev, heads_local, HD)
    value_low = (dot(att_in, w_value) * d_scale).astype(low).reshape(tok_dev, heads_local, HD)
    query_hat, query_inv = norm_parts(query_raw)
    key_hat, key_inv = norm_parts(key_raw)
    query_rot = rotate(query_hat * gain_q, row_cosine, row_sine).astype(low)
    key_rot = rotate(key_hat * gain_k, cosine, sine).astype(low)

    scores = (
        jnp.einsum("qhd,khd->hqk", query_rot, key_rot, preferred_element_type=wide) * att_scale
    )
    allowed = (places[None, :] <= my_rows[:, None]) & (
        segment_ids[None, :] == row_segments[:, None]
    )
    scores = jnp.where(allowed[None], scores, -1e30)
    row_max = jnp.max(scores, axis=-1, keepdims=True)
    expo = jnp.exp(scores - row_max)
    probs = expo / jnp.sum(expo, axis=-1, keepdims=True)
    probs_low = probs.astype(low)
    att_out = (
        jnp.einsum("hqk,khd->qhd", probs_low, value_low, preferred_element_type=wide)
        .reshape(loss_dev, group_width)
        .astype(low)
    )
    hidden = row_embedded + pair_sum(contract_last(att_out, w_out) * att_mult)

    moe_hat, moe_inv = norm_parts(hidden)
    moe_in = (moe_hat * gain_moe).astype(low)
    router_probs = jax.nn.softmax(dot(moe_in, router_low) * d_scale, axis=-1)
    route_any = jnp.any(
        routes[:, :, None] == jnp.arange(expert_count, dtype=jnp.int32)[None, None, :], axis=1
    )
    row_routed = dot(row_sel, route_any.astype(low)) > 0.5
    row_gates = jnp.where(row_routed, router_probs, 0.0)
    relative = jnp.bitwise_xor(dp_rank, jnp.arange(dp_size, dtype=jnp.int32))
    gate_cols = lax.all_to_all(
        jnp.transpose(row_gates)[:, None, :], "dp", split_axis=0, concat_axis=0, tiled=True
    ).reshape(dp_size, loss_dev)
    gate_all = jnp.take(gate_cols, relative, axis=0).reshape(nloss, 1)
    moe_all = gather_rows(moe_in, dp_size, tensor_rank)
    exp_low = exp_w[0].astype(low)
    gate_val = dot(moe_all, exp_low[0]) * d_scale
    up_val = dot(moe_all, exp_low[1]) * d_scale
    sigma = jax.nn.sigmoid(gate_val)
    activated = gate_val * sigma
    middle = (activated * up_val).astype(low)
    expert_out = (contract_last(middle, exp_low[2]) * down_scale).astype(low)
    moe_sum = scatter_rows(gate_all * expert_out.astype(wide), dp_size, tensor_rank)
    after_moe = hidden + moe_scale * moe_sum

    fin_hat, fin_inv = norm_parts(after_moe)
    final_low = (fin_hat * gain_fin).astype(low)
    all_rows = gather_rows(final_low, dp_size, tensor_rank)
    loss_places = jnp.take(loss_rows.reshape(dp_size, loss_dev), relative, axis=0)
    targets = jnp.take(token_ids, relative[:, None] * tok_dev + loss_places + 1).reshape(-1)
    valid_all = valid_mask.astype(wide)
    count = jnp.sum(valid_all)
    row_weight = (
        jnp.take(valid_all.reshape(dp_size, loss_dev), relative, axis=0).reshape(-1) / count
    )
    head_low = head_w.astype(low)
    logits = contract_last(all_rows, head_low) * d_scale
    vocab_start = (dp_rank * tensor_size + tensor_rank) * vocab_local
    target_hot = (
        targets[:, None] == (vocab_start + jnp.arange(vocab_local, dtype=jnp.int32))[None, :]
    )
    local_max = jnp.max(logits, axis=1)
    local_sum = jnp.sum(jnp.exp(logits - local_max[:, None]), axis=1)
    local_target = jnp.sum(jnp.where(target_hot, logits, 0.0), axis=1)

    def merge(first, second):
        larger = jnp.maximum(first[0], second[0])
        summed = first[1] * jnp.exp(first[0] - larger) + second[1] * jnp.exp(second[0] - larger)
        return jnp.stack([larger, summed, first[2] + second[2]])

    stats = jnp.stack([local_max, local_sum, local_target])
    stats = merge(stats, swap_tensor(stats))
    for bit in bits_of(dp_size):
        got = swap_dp(stats, bit, dp_size)
        got = got.reshape(3, -1, 2, bit * loss_dev)
        got = jnp.concatenate([got[:, :, 1:], got[:, :, :1]], axis=2).reshape(3, nloss)
        stats = merge(stats, got)
    log_sum = stats[0] + jnp.log(stats[1])
    loss_here = jnp.sum(row_weight * (log_sum - stats[2]))
    d_logits = (
        row_weight[:, None] * (jnp.exp(logits - log_sum[:, None]) - target_hot.astype(wide))
    ).astype(low)
    d_rows = scatter_rows(dot(d_logits, head_low) * d_scale, dp_size, tensor_rank)
    head_grad = contract_first(d_logits, all_rows) * d_scale
    d_after, fin_gain_grad = norm_back(fin_hat, fin_inv, gain_fin, d_rows)

    d_after_all = gather_rows(d_after.astype(low), dp_size, tensor_rank).astype(wide)
    d_out = (moe_scale * gate_all * d_after_all).astype(low)
    d_gate_here = moe_scale * jnp.sum(expert_out.astype(wide) * d_after_all, axis=1)
    d_middle = dot(d_out, exp_low[2]) * down_scale
    d_gate = (d_middle * up_val * sigma * (1.0 + gate_val * (1.0 - sigma))).astype(low)
    d_up = (d_middle * activated).astype(low)
    d_pairs = (
        (contract_last(d_gate, exp_low[0]) + contract_last(d_up, exp_low[1])) * d_scale
    ).astype(low)
    d_moe_in = scatter_rows(d_pairs.astype(wide), dp_size, tensor_rank)
    down_grad = contract_first(d_out, middle) * down_scale
    gate_grad = contract_first(moe_all, d_gate) * d_scale
    up_grad = contract_first(moe_all, d_up) * d_scale
    d_gate_rows = jnp.take(
        pair_sum_wide(d_gate_here).reshape(dp_size, loss_dev), relative, axis=0
    )
    d_gate_back = lax.all_to_all(
        d_gate_rows[:, None, :], "dp", split_axis=0, concat_axis=0, tiled=True
    ).reshape(dp_size, loss_dev)
    d_probs = jnp.where(row_routed, jnp.transpose(d_gate_back), 0.0)
    d_router = (
        router_probs * (d_probs - jnp.sum(router_probs * d_probs, axis=-1, keepdims=True))
    ).astype(low)
    d_moe_in = d_moe_in + contract_last(d_router, router_low) * d_scale
    d_hidden_part, moe_gain_grad = norm_back(moe_hat, moe_inv, gain_moe, d_moe_in)
    d_hidden = d_after + d_hidden_part

    d_branch = d_hidden.astype(low)
    out_proj_grad = contract_first(d_branch, att_out) * att_mult
    d_att_out = (dot(d_branch, w_out) * att_mult).astype(low).reshape(loss_dev, heads_local, HD)
    d_value = jnp.einsum("hqk,qhd->khd", probs_low, d_att_out, preferred_element_type=wide)
    d_probs_att = jnp.einsum("qhd,khd->hqk", d_att_out, value_low, preferred_element_type=wide)
    delta = jnp.sum(probs * d_probs_att, axis=-1, keepdims=True)
    d_scores = (probs * (d_probs_att - delta)).astype(low)
    d_query_rot = (
        jnp.einsum("hqk,khd->qhd", d_scores, key_rot, preferred_element_type=wide) * att_scale
    )
    d_key_rot = (
        jnp.einsum("hqk,qhd->khd", d_scores, query_rot, preferred_element_type=wide) * att_scale
    )
    d_query_raw, query_gain_grad = norm_back(
        query_hat, query_inv, gain_q, rotate(d_query_rot, row_cosine, -row_sine)
    )
    d_key_raw, key_gain_grad = norm_back(key_hat, key_inv, gain_k, rotate(d_key_rot, cosine, -sine))
    d_query = d_query_raw.reshape(loss_dev, group_width).astype(low)
    d_key = d_key_raw.reshape(tok_dev, group_width).astype(low)
    d_val = d_value.reshape(tok_dev, group_width).astype(low)
    d_att_in = d_scale * (
        contract_last(contract_first(row_sel, d_query).astype(low), w_query)
        + contract_last(d_key, w_key)
        + contract_last(d_val, w_value)
    )
    d_in_first, d_in_second = d_att_in[:tok_half].astype(low), d_att_in[tok_half:].astype(low)
    keep = jnp.where(tensor_rank == 0, d_in_first, d_in_second)
    send = jnp.where(tensor_rank == 0, d_in_second, d_in_first)
    d_in_half = keep.astype(wide) + swap_tensor(send).astype(wide)
    half_start = tensor_rank * tok_half
    hat_half = lax.dynamic_slice_in_dim(att_hat, half_start, tok_half, 0)
    inv_half = lax.dynamic_slice_in_dim(att_inv, half_start, tok_half, 0)
    d_embed_part, att_gain_half = norm_back(hat_half, inv_half, gain_att, d_in_half)
    sel_half = lax.dynamic_slice_in_dim(row_hot.astype(wide), half_start, tok_half, 1)
    d_hidden_half = lax.dot_general(
        sel_half, d_hidden, (((0,), (0,)), ((), ())), precision=highest,
        preferred_element_type=wide,
    )
    d_embedded = (d_hidden_half + d_embed_part).astype(low)
    back = lax.all_to_all(
        d_embedded.reshape(tok_half, dp_size, own_width),
        "dp", split_axis=1, concat_axis=0, tiled=True,
    ).reshape(dp_size, tok_half, own_width)
    back_columns = pair_join(back, tensor_rank, 1).reshape(-1, own_width)
    emb_grad = jax.ops.segment_sum(
        back_columns.astype(wide), token_ids, num_segments=emb_w.shape[0]
    )

    att_grad_full = jnp.concatenate(
        [
            contract_first(row_in, d_query) * d_scale,
            contract_first(att_in, d_key) * d_scale,
            contract_first(att_in, d_val) * d_scale,
            out_proj_grad,
        ],
        axis=1,
    ).astype(low)
    att_parts = lax.all_to_all(
        att_grad_full.reshape(dp_size, row_own, 4 * group_width),
        "dp", split_axis=0, concat_axis=0, tiled=True,
    )
    att_grad = jnp.sum(att_parts.astype(wide), axis=0).reshape(row_own, 4, group_width)
    zero_row = jnp.zeros((width,), wide)
    once = jnp.where(tensor_rank == 0, 1.0, 0.0)
    query_gain_full = lax.dynamic_update_slice_in_dim(
        zero_row, query_gain_grad.reshape(group_width), tensor_rank * group_width, 0
    )
    key_gain_full = lax.dynamic_update_slice_in_dim(
        zero_row, key_gain_grad.reshape(group_width), tensor_rank * group_width, 0
    )
    router_grad = contract_first(d_router, moe_in) * d_scale
    small_grad_full = pair_sum_wide(
        jnp.concatenate(
            [
                once * router_grad,
                jnp.stack(
                    [
                        att_gain_half,
                        query_gain_full,
                        key_gain_full,
                        once * moe_gain_grad,
                        once * fin_gain_grad,
                    ]
                ),
            ],
            axis=0,
        )
    )
    small_parts = lax.all_to_all(
        jnp.transpose(small_grad_full.reshape(expert_count + 5, dp_size, row_own), (1, 0, 2)),
        "dp", split_axis=0, concat_axis=0, tiled=True,
    )
    small_grad = jnp.transpose(jnp.sum(small_parts, axis=0))

    exp_grad = jnp.stack([gate_grad, up_grad, down_grad], axis=0)
    local_squares = (
        jnp.sum(exp_grad * exp_grad) + jnp.sum(head_grad * head_grad) + jnp.sum(att_grad * att_grad)
    )
    local_squares = (
        local_squares
        + (jnp.sum(emb_grad * emb_grad) + jnp.sum(small_grad * small_grad)) / tensor_size
    )
    first_device = (dp_rank == 0) & (tensor_rank == 0)
    totals = jnp.stack([local_squares, jnp.where(first_device, loss_here, 0.0)])
    totals = totals + swap_tensor(totals)
    for bit in bits_of(dp_size):
        totals = totals + swap_dp(totals, bit, dp_size)
    loss = totals[1]
    grad_norm = jnp.sqrt(totals[0])
    clip = jnp.minimum(1.0, 2.0 * nloss ** (-0.5) / (grad_norm + 1e-06))
    count_t = step_count[0].astype(wide)
    att_moment = 0.5 * att_mom + clip * att_grad
    outgoing = jnp.zeros((dp_size, row_own, group_width), low)
    outgoing = lax.dynamic_update_slice_in_dim(
        outgoing, jnp.transpose(att_moment, (1, 0, 2)).astype(low), 0, 0
    )
    owned_block = lax.all_to_all(
        outgoing, "dp", split_axis=0, concat_axis=0, tiled=True
    ).astype(wide)
    owned_ortho = orthogonal_rows(
        owned_block.reshape(dp_size * row_own, 1, group_width), gram_local
    )
    returned_rows = lax.all_to_all(
        owned_ortho.reshape(dp_size, row_own, group_width).astype(low),
        "dp", split_axis=0, concat_axis=0, tiled=True,
    ).astype(wide)
    att_ortho = jnp.transpose(returned_rows[:4], (1, 0, 2))
    att_update = -0.3 * (width**0.5 * att_ortho + 0.1 * att_w)
    emb_out = adam_step(emb_w, emb_m, emb_v, clip * emb_grad, count_t)
    head_out = adam_step(head_w, head_m, head_v, clip * head_grad, count_t)
    small_out = adam_step(small_w, small_m, small_v, clip * small_grad, count_t)
    exp_moment = 0.5 * exp_mom + clip * exp_grad[None]
    exp_ortho = jnp.transpose(
        orthogonal_rows(jnp.transpose(exp_moment[0], (1, 0, 2)), gram_local), (1, 0, 2)
    )[None]
    exp_update = -0.3 * (width**0.5 * exp_ortho + 0.1 * exp_w)
    return (
        loss,
        grad_norm,
        emb_out[0],
        emb_out[1],
        emb_out[2],
        emb_out[3],
        head_out[0],
        head_out[1],
        head_out[2],
        head_out[3],
        att_update,
        att_moment,
        (att_w + att_update).astype(jnp.bfloat16),
        exp_update,
        exp_moment,
        (exp_w + exp_update).astype(jnp.bfloat16),
        small_out[0],
        small_out[1],
        small_out[2],
        small_out[3],
    )


def solution(mesh):
    in_specs = (
        P(),
        P("dp"),
        P("dp", None),
        P(),
        P(),
        P(),
        P(None, "dp"),
        P(None, "dp"),
        P(None, "dp"),
        P(("dp", "tensor"), None),
        P(("dp", "tensor"), None),
        P(("dp", "tensor"), None),
        P("dp", None, "tensor"),
        P("dp", None, "tensor"),
        P("dp", None, None, "tensor"),
        P("dp", None, None, "tensor"),
        P("dp", None),
        P("dp", None),
        P("dp", None),
    )
    out_specs = (
        P(),
        P(),
        P(None, "dp"),
        P(None, "dp"),
        P(None, "dp"),
        P(None, "dp"),
        P(("dp", "tensor"), None),
        P(("dp", "tensor"), None),
        P(("dp", "tensor"), None),
        P(("dp", "tensor"), None),
        P("dp", None, "tensor"),
        P("dp", None, "tensor"),
        P("dp", None, "tensor"),
        P("dp", None, None, "tensor"),
        P("dp", None, None, "tensor"),
        P("dp", None, None, "tensor"),
        P("dp", None),
        P("dp", None),
        P("dp", None),
        P("dp", None),
    )
    return jax.shard_map(
        per_device, mesh=mesh, in_specs=in_specs, out_specs=out_specs, check_vma=False
    )
```
